32 devices in a mesh: freq: 16 (over z, y, core), chan: 2 (over x).
Axes of the slice: x: 2, y: 2, z: 4, core: 2. Of those that a mesh axis runs over, the one named last changes fastest.
Arguments:
- traces: bfloat16 [256, 2048, 256], P('freq', 'chan'), may hold values from -6 to 6
- channel_mask: int32 [2048], P('chan'), may hold values 0 or 1
- bin_index: int32 [16], replicated, may hold values from 1 to 127
Outputs:
- cross: bfloat16 [16, 2, 2048, 2048], P('freq', None, 'chan')
The draws below stay inside these ranges and needn't reach their ends.
All inputs are finite; a program needn't handle non-finite values. No bound on the sum of `channel_mask` on one device may be relied on, other than what follows from the above.
Results may differ from the reference program's by a relative error of at most 0.0064.
Values may be sent and summed in bfloat16 or wider, within the bound.
No kernel may reach another device: no remote copies, remote signals or barrier semaphores. Data moves between devices by JAX's collectives and lax.ppermute only.
A program may use at most 64 MiB of HBM per device.

```python
import math
import jax
import jax.numpy as jnp
from jax import lax

CH = 2048
L = 256
SEG = 256
BINS = 16


def touch_ends(drawn, key, least, top_value):
    spot = [jax.random.randint(jax.random.fold_in(key, axis), (), 0, length) for axis, length in enumerate(drawn.shape)]
    main_axis = drawn.shape.index(max(drawn.shape))
    beside = spot[:main_axis] + [(spot[main_axis] + 1) % drawn.shape[main_axis]] + spot[main_axis + 1:]
    return drawn.at[tuple(spot)].set(least).at[tuple(beside)].set(top_value)


def block_scale(key, dims, cuts, least, largest):
    def one(dim, parts):
        heights = jax.random.uniform(jax.random.fold_in(jax.random.fold_in(key, 6), dim), (parts,), jnp.float32, least / len(cuts), largest / len(cuts))
        return jnp.repeat(jnp.exp(heights), dims[dim] // parts).reshape((-1,) + (1,) * (len(dims) - dim - 1))

    loudness = one(*cuts[0])
    for cut in cuts[1:]:
        loudness = loudness * one(*cut)
    return loudness


def noise(key, extent, scale, limit, cuts=(), kind=jnp.bfloat16):
    drawn = scale * jax.random.normal(key, extent, jnp.float32)
    if cuts:
        drawn = drawn * block_scale(key, extent, cuts, -0.22, 0.18)
    return jnp.clip(drawn, -limit, limit).astype(kind)


def setup_inputs(seed: int = 0) -> dict:
    keys = jax.random.split(jax.random.key(seed), 4)
    return {
        "traces": noise(keys[0], (SEG, CH, L), 1.0, 6.0, ((0, 16), (1, 2))),
        "channel_mask": touch_ends((jax.random.randint(keys[1], (CH,), 0, 8) < 7).astype(jnp.int32), jax.random.fold_in(keys[1], 1), 0, 1),
        "bin_index": touch_ends(jax.random.randint(keys[2], (BINS,), 1, L // 2), jax.random.fold_in(keys[2], 1), 1, (L // 2) - 1).astype(jnp.int32),
    }


def reference(traces, channel_mask, bin_index):
    segments, channels, length = traces.shape
    nbins = bin_index.shape[0]
    samples = jnp.arange(length, dtype=jnp.int32)
    phase_index = bin_index[None, :] * samples[:, None] % length
    angles = 2.0 * math.pi / length * phase_index.astype(jnp.float32)
    wave_table = jnp.stack([jnp.cos(angles), -jnp.sin(angles)], axis=2).reshape(length, 2 * nbins).astype(jnp.bfloat16)
    taper_curve = 0.5 - 0.5 * jnp.cos(2.0 * math.pi / length * (samples.astype(jnp.float32) + 0.5))
    channel_gain = channel_mask.astype(jnp.float32)

    def one_segment(record):
        spectral_values = record.astype(jnp.float32)
        spread = jnp.sqrt(lax.optimization_barrier(jnp.mean(spectral_values * spectral_values, axis=1, keepdims=True)) + 1e-06)
        tapered = (spectral_values / spread * taper_curve[None, :] * channel_gain[:, None]).astype(jnp.bfloat16)
        return jnp.dot(tapered, wave_table, preferred_element_type=jnp.float32)
    segment_spectra = lax.map(one_segment, traces)
    segment_spectra = segment_spectra.reshape(segments, channels, nbins, 2).transpose(2, 0, 3, 1)
    band_power = lax.optimization_barrier(jnp.sum(segment_spectra * segment_spectra, axis=(1, 2))) / segments + 1e-06
    whitened = (segment_spectra / jnp.sqrt(band_power)[:, None, None, :]).astype(jnp.bfloat16)
    inverse = 1.0 / segments

    def one_bin(spectrum):
        real_rows = spectrum.reshape(2 * segments, channels)
        turned = jnp.stack([spectrum[:, 1], -spectrum[:, 0]], axis=1).reshape(2 * segments, channels)
        stacked_spectra = jnp.concatenate([real_rows, turned], axis=1)
        cross_product_term = lax.dot_general(stacked_spectra, real_rows, (((0,), (0,)), ((), ())), preferred_element_type=jnp.float32)
        return (cross_product_term * inverse).reshape(2, channels, channels).astype(jnp.bfloat16)
    return lax.map(one_bin, whitened)
```

```python
import functools
import math

import jax
import jax.numpy as jnp
from jax import lax
from jax.experimental import pallas as pl
from jax.experimental.pallas import tpu as pltpu
from jax.sharding import PartitionSpec as P

LANES = 128
SHARES = (5, 3)


def passed_along(value, axis, steps):
    count = lax.axis_size(axis)
    pairs = [(source, (source + steps) % count) for source in range(count)]
    return lax.ppermute(value, axis, pairs)


def divisor(value, limit):
    return max(d for d in range(1, min(value, limit) + 1) if value % d == 0)


def pieces(width):
    units = width // LANES
    if units < 2:
        return [(0, width)]
    first = min(max(1, round(units * SHARES[0] / sum(SHARES))), units - 1)
    return [(0, first * LANES), (first * LANES, width - first * LANES)]


def spectra_kernel(batch, segments, table_ref, taper_ref, gain_ref, traces_ref, out_ref, held):
    step = pl.program_id(0)
    rows, length = table_ref.shape
    taper = taper_ref[...]
    for place in range(batch):
        record = traces_ref[place].astype(jnp.float32)
        squares = jnp.sum(record * record, axis=1, keepdims=True)
        inverse = lax.rsqrt(squares / length + 1e-06)
        tapered = (record * inverse * taper).astype(jnp.bfloat16)
        spectra = lax.dot_general(
            table_ref[...], tapered, (((1,), (1,)), ((), ())), preferred_element_type=jnp.float32
        )
        spectra = spectra * gain_ref[...]
        for tile in range(held.shape[0]):
            kept = spectra[:, tile * LANES : (tile + 1) * LANES]
            held[tile, pl.ds(step * batch + place, rows, stride=segments), :] = kept

    @pl.when(step == pl.num_programs(0) - 1)
    def _():
        for tile in range(held.shape[0]):
            out_ref[:, tile * LANES : (tile + 1) * LANES] = held[tile].astype(jnp.bfloat16)


def spectra_of(traces, gain, table, taper, start, size):
    segments, width, length = traces.shape
    rows = table.shape[0]
    batch = divisor(segments, 4)
    return pl.pallas_call(
        functools.partial(spectra_kernel, batch, segments),
        grid=(segments // batch,),
        in_specs=[
            pl.BlockSpec((rows, length), lambda i: (0, 0)),
            pl.BlockSpec((1, length), lambda i: (0, 0)),
            pl.BlockSpec((pl.Element(1), pl.Element(size)), lambda i: (0, start)),
            pl.BlockSpec(
                (pl.Element(batch), pl.Element(size), pl.Element(length)),
                lambda i: (i * batch, start, 0),
            ),
        ],
        out_specs=pl.BlockSpec((rows * segments, size), lambda i: (0, 0)),
        out_shape=jax.ShapeDtypeStruct((rows * segments, size), jnp.bfloat16),
        scratch_shapes=[pltpu.VMEM((size // LANES, rows * segments, LANES), jnp.float32)],
        cost_estimate=pl.CostEstimate(
            flops=2 * rows * segments * size * length,
            bytes_accessed=2 * segments * size * length,
            transcendentals=0,
        ),
    )(table, taper, gain, traces)


def column_scale(values, segments):
    wide = values.astype(jnp.float32)
    return lax.rsqrt(jnp.sum(wide * wide, axis=0, keepdims=True) / segments + 1e-06)


def row_scale(values, segments):
    wide = values.astype(jnp.float32)
    return lax.rsqrt(jnp.sum(wide * wide, axis=1, keepdims=True) / segments + 1e-06)


def own_kernel(local, segments, count, place_ref, *refs):
    own_refs, (out_ref, left_ref, whole, across) = refs[:count], refs[count:]
    step = pl.program_id(0)

    @pl.when(step == 0)
    def _():
        start = 0
        for ref in own_refs:
            size = ref.shape[1]
            whole[:, start : start + size] = ref[...]
            start += size
        across[...] = column_scale(whole[...], segments)

    rows = out_ref.shape[2]
    block = whole[:, pl.ds(pl.multiple_of(step * rows, rows), rows)]
    parts = block.reshape(block.shape[0] // (2 * local), 2, local, rows)
    turned = jnp.concatenate([parts[:, 1:], -parts[:, :1]], axis=1).reshape(block.shape)
    plain_left = block.T
    turned_left = turned.T
    left_ref[0] = plain_left
    left_ref[1] = turned_left
    scale = row_scale(plain_left, segments) * (1.0 / segments)
    for part, left in enumerate((plain_left, turned_left)):
        product = jnp.dot(left, whole[...], preferred_element_type=jnp.float32)
        out_ref[0, part] = (product * scale * across[...]).astype(jnp.bfloat16)


def own_blocks(own, local, place, bins_local, group):
    depth = own[0].shape[0]
    width = sum(piece.shape[1] for piece in own)
    segments = depth // 2
    rows = divisor(width, 256)
    return pl.pallas_call(
        functools.partial(own_kernel, local, segments, len(own)),
        grid_spec=pltpu.PrefetchScalarGridSpec(
            num_scalar_prefetch=1,
            grid=(width // rows,),
            in_specs=[pl.BlockSpec(piece.shape, lambda i, at: (0, 0)) for piece in own],
            out_specs=[
                pl.BlockSpec((1, 2, rows, width), lambda i, at: (0, 0, i, at[0])),
                pl.BlockSpec((2, rows, depth), lambda i, at: (0, i, 0)),
            ],
            scratch_shapes=[pltpu.VMEM((depth, width), jnp.bfloat16), pltpu.VMEM((1, width), jnp.float32)],
        ),
        out_shape=[
            jax.ShapeDtypeStruct((bins_local, 2, width, group * width), jnp.bfloat16),
            jax.ShapeDtypeStruct((2, width, depth), jnp.bfloat16),
        ],
        cost_estimate=pl.CostEstimate(
            flops=4 * width * width * depth, bytes_accessed=4 * width * width, transcendentals=0
        ),
    )(place, *own)


def peer_kernel(segments, place_ref, left_ref, peer_ref, result_ref, out_ref, across):
    @pl.when(pl.program_id(0) == 0)
    def _():
        across[...] = column_scale(peer_ref[...], segments)

    scale = row_scale(left_ref[0], segments) * (1.0 / segments)
    for part in range(2):
        product = jnp.dot(left_ref[part], peer_ref[...], preferred_element_type=jnp.float32)
        out_ref[0, part] = (product * scale * across[...]).astype(jnp.bfloat16)


def peer_blocks(result, left, peer, place, unit):
    depth, size = peer.shape
    width = left.shape[1]
    rows = divisor(width, 256)
    return pl.pallas_call(
        functools.partial(peer_kernel, depth // 2),
        grid_spec=pltpu.PrefetchScalarGridSpec(
            num_scalar_prefetch=1,
            grid=(width // rows,),
            in_specs=[
                pl.BlockSpec((2, rows, depth), lambda i, at: (0, i, 0)),
                pl.BlockSpec((depth, size), lambda i, at: (0, 0)),
                pl.BlockSpec(memory_space=pl.ANY),
            ],
            out_specs=pl.BlockSpec(
                (pl.Element(1), pl.Element(2), pl.Element(rows), pl.Element(size)),
                lambda i, at: (0, 0, i * rows, pl.multiple_of(at[0] * unit, unit)),
            ),
            scratch_shapes=[pltpu.VMEM((1, size), jnp.float32)],
        ),
        out_shape=jax.ShapeDtypeStruct(result.shape, result.dtype),
        input_output_aliases={3: 0},
        cost_estimate=pl.CostEstimate(
            flops=4 * width * size * depth, bytes_accessed=4 * width * size, transcendentals=0
        ),
    )(place, left, peer, result)


def shards(traces, channel_mask, bin_index):
    local, width, length = traces.shape
    nbins = bin_index.shape[0]
    samples = jnp.arange(length, dtype=jnp.int32)
    phase_index = bin_index[:, None, None] * samples[None, None, :] % length
    angles = 2.0 * math.pi / length * phase_index.astype(jnp.float32)
    real_part = jnp.arange(2, dtype=jnp.int32)[None, :, None] == 0
    table = jnp.where(real_part, jnp.cos(angles), -jnp.sin(angles))
    table = table.reshape(2 * nbins, length).astype(jnp.bfloat16)
    taper = 0.5 - 0.5 * jnp.cos(2.0 * math.pi / length * (samples.astype(jnp.float32) + 0.5))
    gain = channel_mask.astype(jnp.float32)[None, :]

    freq = lax.axis_size("freq")
    group = lax.axis_size("chan")
    own_index = lax.axis_index("chan")
    assert nbins == freq
    cuts = pieces(width)
    own = []
    for start, size in cuts:
        spectra = spectra_of(traces, gain, table, taper[None, :], start, size)
        blocks = spectra.reshape(nbins, 2 * local, size)
        arrived = lax.all_to_all(blocks, "freq", split_axis=0, concat_axis=0, tiled=True)
        own.append(arrived.reshape(freq * 2 * local, size))
    result, left = own_blocks(own, local, own_index[None].astype(jnp.int32), 1, group)
    moving = own
    for step in range(1, group):
        moving = [passed_along(piece, "chan", 1) for piece in moving]
        owner = (own_index - step) % group
        for (start, size), piece in zip(cuts, moving):
            unit = math.gcd(start, width)
            place = (owner * width + start) // unit
            result = peer_blocks(result, left, piece, place[None].astype(jnp.int32), unit)
    return result


def solution(mesh):
    in_specs = (P("freq", "chan", None), P("chan"), P())
    out_specs = P("freq", None, "chan", None)
    return jax.shard_map(shards, mesh=mesh, in_specs=in_specs, out_specs=out_specs, check_vma=False)
```

```python
import functools
import math

import jax
import jax.numpy as jnp
from jax import lax
from jax.experimental import pallas as pl
from jax.experimental.pallas import tpu as pltpu
from jax.sharding import PartitionSpec as P

LANES = 128
GROUPS = 8
VMEM_LIMIT = 20 * 2**20


def passed_along(value, axis, steps):
    count = lax.axis_size(axis)
    pairs = [(source, (source + steps) % count) for source in range(count)]
    return lax.ppermute(value, axis, pairs)


def swapped(value, axis, mask):
    count = lax.axis_size(axis)
    return lax.ppermute(value, axis, [(source, source ^ mask) for source in range(count)])


def divisor(value, limit):
    return max(d for d in range(1, min(value, limit) + 1) if value % d == 0)


def transfer_order(pairs):
    quarter = pairs // 4
    if quarter == 0:
        return list(range(1, pairs))
    far, near, corner = (range(quarter * k, quarter * (k + 1)) for k in (2, 1, 3))
    return [*far, *range(1, quarter), *near, *corner]


def arrival_order(pairs):
    quarter = pairs // 4
    if quarter == 0:
        return list(range(pairs))
    return [k for block in (0, 2, 1, 3) for k in range(quarter * block, quarter * (block + 1))]


def spectra_kernel(batch, segments, bins_ref, index_ref, gain_ref, traces_ref, keep_ref, send_ref, table, taper, held):
    step = pl.program_id(0)
    rows, length = table.shape
    nbins = rows // 2

    @pl.when(step == 0)
    def _():
        row = lax.broadcasted_iota(jnp.int32, (rows, length), 0)
        sample = lax.broadcasted_iota(jnp.int32, (rows, length), 1)
        bins = jnp.zeros((rows, length), jnp.int32)
        for k in range(nbins):
            core, pair = divmod(k, nbins // 2)
            bins = jnp.where(row // 2 == k, bins_ref[index_ref[0] ^ (2 * pair + core)], bins)
        phase = (bins * sample) & (length - 1)
        angle = 2.0 * math.pi / length * phase.astype(jnp.float32)
        wave = jnp.where(row % 2 == 0, jnp.cos(angle), -jnp.sin(angle))
        table[...] = wave.astype(jnp.bfloat16)
        place = lax.broadcasted_iota(jnp.int32, (8, length), 1).astype(jnp.float32)
        curve = 0.5 - 0.5 * jnp.cos(2.0 * math.pi / length * (place + 0.5))
        taper[...] = curve * math.sqrt(length)

    gain = gain_ref[...].astype(jnp.float32)
    for place in range(batch):
        record = traces_ref[place].astype(jnp.float32)
        squares = jnp.sum(record * record, axis=1, keepdims=True)
        inverse = lax.rsqrt(squares + 1e-06 * length)
        tapered = (record * inverse * taper[:1]).astype(jnp.bfloat16)
        spectra = lax.dot_general(
            table[...], tapered, (((1,), (1,)), ((), ())), preferred_element_type=jnp.float32
        )
        spectra = spectra * gain
        for tile in range(held.shape[0]):
            kept = spectra[:, tile * LANES : (tile + 1) * LANES]
            held[tile, pl.ds(step * batch + place, rows, stride=segments), :] = kept

    @pl.when(step == pl.num_programs(0) - 1)
    def _():
        half = rows * segments // 2
        for tile in range(held.shape[0]):
            lanes = slice(tile * LANES, (tile + 1) * LANES)
            keep_ref[:, lanes] = held[tile, :half].astype(jnp.bfloat16)
            send_ref[:, lanes] = held[tile, half:].astype(jnp.bfloat16)


def spectra_of(traces, channel_mask, bin_index, index):
    segments, width, length = traces.shape
    assert length & (length - 1) == 0
    rows = 2 * bin_index.shape[0]
    batch = divisor(segments, 2)
    half = jax.ShapeDtypeStruct((rows * segments // 2, width), jnp.bfloat16)
    return pl.pallas_call(
        functools.partial(spectra_kernel, batch, segments),
        grid_spec=pltpu.PrefetchScalarGridSpec(
            num_scalar_prefetch=2,
            grid=(segments // batch,),
            in_specs=[
                pl.BlockSpec((1, width), lambda i, *_: (0, 0)),
                pl.BlockSpec((batch, width, length), lambda i, *_: (i, 0, 0)),
            ],
            out_specs=[pl.BlockSpec(half.shape, lambda i, *_: (0, 0))] * 2,
            scratch_shapes=[
                pltpu.VMEM((rows, length), jnp.bfloat16),
                pltpu.VMEM((8, length), jnp.float32),
                pltpu.VMEM((width // LANES, rows * segments, LANES), jnp.float32),
            ],
        ),
        out_shape=[half, half],
        compiler_params=pltpu.CompilerParams(vmem_limit_bytes=VMEM_LIMIT),
        cost_estimate=pl.CostEstimate(
            flops=2 * rows * segments * width * length,
            bytes_accessed=2 * segments * width * length,
            transcendentals=0,
        ),
    )(bin_index, index, channel_mask[None, :], traces)


def gathered(refs, whole, across, segments):
    start = 0
    for ref in refs:
        whole[start : start + ref.shape[0]] = ref[...]
        start += ref.shape[0]
    wide = whole[...].astype(jnp.float32)
    across[...] = lax.rsqrt(jnp.sum(wide * wide, axis=0, keepdims=True) / segments + 1e-06)


def row_scale(values, segments):
    wide = values.astype(jnp.float32)
    power = jnp.sum(wide * wide, axis=1, keepdims=True) / segments
    return lax.rsqrt(power + 1e-06) * (1.0 / segments)


def own_kernel(local, segments, count, place_ref, *refs):
    own_refs, (out_ref, left_ref, whole, across) = refs[:count], refs[count:]
    step = pl.program_id(0)

    @pl.when(step == 0)
    def _():
        gathered(own_refs, whole, across, segments)

    rows = out_ref.shape[2]
    block = whole[:, pl.ds(pl.multiple_of(step * rows, rows), rows)]
    parts = block.reshape(block.shape[0] // (2 * local), 2, local, rows)
    turned = jnp.concatenate([parts[:, 1:], -parts[:, :1]], axis=1).reshape(block.shape)
    plain_left = block.T
    turned_left = turned.T
    here = pl.ds(pl.multiple_of(step * rows, rows), rows)
    left_ref[0, here] = plain_left
    left_ref[1, here] = turned_left
    scale = row_scale(plain_left, segments)
    for part, left in enumerate((plain_left, turned_left)):
        product = jnp.dot(left, whole[...], preferred_element_type=jnp.float32)
        out_ref[0, part] = (product * scale * across[...]).astype(jnp.bfloat16)


def own_blocks(own, local, place, group):
    depth = sum(piece.shape[0] for piece in own)
    width = own[0].shape[1]
    rows = divisor(width, 256)
    return pl.pallas_call(
        functools.partial(own_kernel, local, depth // 2, len(own)),
        grid_spec=pltpu.PrefetchScalarGridSpec(
            num_scalar_prefetch=1,
            grid=(width // rows,),
            in_specs=[pl.BlockSpec(memory_space=pltpu.VMEM)] * len(own),
            out_specs=[
                pl.BlockSpec((1, 2, rows, width), lambda i, at: (0, 0, i, at[0])),
                pl.BlockSpec(memory_space=pltpu.VMEM),
            ],
            scratch_shapes=[pltpu.VMEM((depth, width), jnp.bfloat16), pltpu.VMEM((1, width), jnp.float32)],
        ),
        out_shape=[
            jax.ShapeDtypeStruct((1, 2, width, group * width), jnp.bfloat16),
            jax.ShapeDtypeStruct((2, width, depth), jnp.bfloat16),
        ],
        compiler_params=pltpu.CompilerParams(vmem_limit_bytes=VMEM_LIMIT),
        cost_estimate=pl.CostEstimate(
            flops=4 * width * width * depth, bytes_accessed=4 * width * width, transcendentals=0
        ),
    )(place, *own)


def peer_kernel(segments, count, place_ref, left_ref, *refs):
    peer_refs, (_, out_ref, whole, across) = refs[:count], refs[count:]
    step = pl.program_id(0)

    @pl.when(step == 0)
    def _():
        gathered(peer_refs, whole, across, segments)

    rows = out_ref.shape[2]
    here = pl.ds(pl.multiple_of(step * rows, rows), rows)
    scale = row_scale(left_ref[0, here], segments)
    for part in range(2):
        product = jnp.dot(left_ref[part, here], whole[...], preferred_element_type=jnp.float32)
        out_ref[0, part] = (product * scale * across[...]).astype(jnp.bfloat16)


def peer_blocks(result, left, peer, place):
    _, width, depth = left.shape
    rows = divisor(width, 256)
    return pl.pallas_call(
        functools.partial(peer_kernel, depth // 2, len(peer)),
        grid_spec=pltpu.PrefetchScalarGridSpec(
            num_scalar_prefetch=1,
            grid=(width // rows,),
            in_specs=[
                *[pl.BlockSpec(memory_space=pltpu.VMEM)] * (1 + len(peer)),
                pl.BlockSpec(memory_space=pl.ANY),
            ],
            out_specs=pl.BlockSpec((1, 2, rows, width), lambda i, at: (0, 0, i, at[0])),
            scratch_shapes=[pltpu.VMEM((depth, width), jnp.bfloat16), pltpu.VMEM((1, width), jnp.float32)],
        ),
        out_shape=jax.ShapeDtypeStruct(result.shape, result.dtype),
        input_output_aliases={2 + len(peer): 0},
        compiler_params=pltpu.CompilerParams(vmem_limit_bytes=VMEM_LIMIT),
        cost_estimate=pl.CostEstimate(
            flops=4 * width * width * depth, bytes_accessed=4 * width * width, transcendentals=0
        ),
    )(place, left, *peer, result)


def shards(traces, channel_mask, bin_index):
    local, width, _ = traces.shape
    nbins = bin_index.shape[0]
    freq = lax.axis_size("freq")
    group = lax.axis_size("chan")
    own_index = lax.axis_index("chan")
    assert nbins == freq and freq & (freq - 1) == 0
    pairs = freq // 2
    depth = 2 * local

    index = lax.axis_index("freq")[None].astype(jnp.int32)
    keep, send = spectra_of(traces, channel_mask, bin_index, index)
    keep = keep.reshape(pairs, depth, width)
    got = swapped(send, "freq", 1).reshape(pairs, depth, width)
    arrived = {}
    for pair in [*transfer_order(pairs), 0]:
        both = jnp.concatenate([keep[pair], got[pair]], axis=0)
        arrived[pair] = swapped(both, "freq", 2 * pair) if pair else both
    order = arrival_order(pairs)
    each = max(1, pairs // GROUPS)
    own = []
    for start in range(0, pairs, each):
        members = [arrived[pair] for pair in order[start : start + each]]
        own.append(members[0] if each == 1 else jnp.concatenate(members, axis=0))
    moving = own
    moved = []
    for _ in range(1, group):
        for place in range(len(moving)):
            moving = [*moving[:place], passed_along(moving[place], "chan", 1), *moving[place + 1 :]]
        moved.append(moving)
    result, left = own_blocks(own, local, own_index[None].astype(jnp.int32), group)
    for step in range(1, group):
        owner = (own_index - step) % group
        result = peer_blocks(result, left, moved[step - 1], owner[None].astype(jnp.int32))
    return result


def solution(mesh):
    in_specs = (P("freq", "chan", None), P("chan"), P())
    out_specs = P("freq", None, "chan", None)
    return jax.shard_map(shards, mesh=mesh, in_specs=in_specs, out_specs=out_specs, check_vma=False)
```
